1024 devices in a mesh: dom: 128 (over x_hi, z, y), band: 8 (over x_lo, core).
Axes of the slice: x: 8 (x_hi: 2, x_lo: 4; x = x_hi * 4 + x_lo), y: 8, z: 8, core: 2. Of those that a mesh axis runs over, the one named last changes fastest.
Arguments:
- filter_input: bfloat16 [165888, 2048], P('dom', 'band'), may hold values from -6 to 6
- element_matrix: bfloat16 [125, 125], replicated, as said below
- cell_scale: float32 [2048], P('dom'), may hold values from 0.5 to 2
- connectivity: int32 [2048, 125], P('dom'), may hold values from 0 to 1376, as said below
- interface_nodes: int32 [10368], P('dom'), may hold values from 0 to 1295, as said below
- lumped_mass: float32 [165888], P('dom'), may hold values from 0.5 to 2
- potential: float32 [165888], P('dom'), may hold values from -1 to 1
Outputs:
- filtered: bfloat16 [165888, 2048], P('dom', 'band')
- intersection: float32 [2048, 2048], P('dom', 'band')
The draws below stay inside these ranges and needn't reach their ends.
Inputs may be any that keep to these rules, and one draw needn't show every extreme that they name: `connectivity`: within a cell the indices are distinct; indices of 1296 and above stand only in a domain's last 4 cells. `interface_nodes`: within one domain's list the nodes are distinct. `element_matrix`: symmetric positive definite: a sum over the three directions of degree-4 Gauss-Lobatto stiffness terms with positive factors, plus a positive diagonal mass term.
All inputs are finite; a program needn't handle non-finite values.
Results may differ from the reference program's by a relative error of at most 0.0081.
The reference program's roundings to bfloat16 on the way (of `middle` and `weighted`) count: a program that leaves them out, or rounds other values in their place, can miss the bound.
Values may be sent and summed in bfloat16 or wider, within the bound.
No kernel may reach another device: no remote copies, remote signals or barrier semaphores. Data moves between devices by JAX's collectives and lax.ppermute only.
A program may use at most 32 MiB of HBM per device.

```python
import math
import jax
import jax.numpy as jnp
import numpy as np
from jax import lax

NODES_PER_CELL = 125
STATES_DEV = 256
CX = 2
CY = 2
LAYERS = 4
IFACE = 81
NODES_DEV = 1296
CELLS_DEV = 16
STATES = 2048
NODES = 165888
CELLS = 2048
N_DOM = 128
N_BAND = 8


def force_pair(order, wanted, slot, active):
    current = order[slot]
    swapped = jnp.where(order == wanted, current, order)
    swapped = swapped.at[slot].set(wanted)
    return jnp.where(active, swapped, order)


def lobatto_tables():
    root_value = np.sqrt(3.0 / 7.0)
    points = np.array([-1.0, -root_value, 0.0, root_value, 1.0])
    weights = np.array([0.1, 49.0 / 90.0, 32.0 / 45.0, 49.0 / 90.0, 0.1])
    barycentric = np.ones(5)
    for first in range(5):
        for second in range(5):
            if first != second:
                barycentric[first] = barycentric[first] / (points[first] - points[second])
    slopes = np.zeros((5, 5))
    for first in range(5):
        for second in range(5):
            if first != second:
                slopes[first, second] = barycentric[second] / barycentric[first] / (points[first] - points[second])
        slopes[first, first] = -np.sum(slopes[first])
    stiffness = slopes.T @ (weights[:, None] * slopes)
    stiffness = 0.5 * (stiffness + stiffness.T)
    return (weights, stiffness)


def draw_element_matrix(key, part):
    weights, stiffness = lobatto_tables()
    diagonal_weights = np.eye(5) * weights[None, :]
    along_x = np.kron(np.kron(stiffness, diagonal_weights), diagonal_weights)
    along_y = np.kron(np.kron(diagonal_weights, stiffness), diagonal_weights)
    along_z = np.kron(np.kron(diagonal_weights, diagonal_weights), stiffness)
    mass_table = np.kron(np.kron(diagonal_weights, diagonal_weights), diagonal_weights)
    total_table = along_x + along_y + along_z
    normalizer = 2.0 * np.max(np.sum(total_table * np.eye(125), axis=1))
    factor_key = jax.random.fold_in(key, 37)
    mass_key = jax.random.fold_in(key, 41)
    factors = jnp.exp(jax.random.uniform(factor_key, (3,), jnp.float32, np.log(0.5), np.log(2.0)))
    mass_factor = jax.random.uniform(mass_key, (), jnp.float32, 0.5, 1.5)
    element = factors[0] * jnp.asarray(along_x / normalizer, jnp.float32)
    element = element + factors[1] * jnp.asarray(along_y / normalizer, jnp.float32)
    element = element + factors[2] * jnp.asarray(along_z / normalizer, jnp.float32)
    element = element + mass_factor * jnp.asarray(mass_table / normalizer, jnp.float32)
    return element.astype(jnp.bfloat16)


def natural_table():
    side_count = 4 * CY + 1
    entries = []
    for layer in range(LAYERS):
        for across in range(CX):
            for along in range(CY):
                cell_nodes = []
                for first in range(5):
                    for second in range(5):
                        for third in range(5):
                            place_x = 4 * across + first
                            place_y = 4 * along + second
                            place_z = 4 * layer + third
                            cell_nodes.append(place_z * IFACE + place_x * side_count + place_y)
                entries.append(cell_nodes)
    return np.array(entries, np.int32)


def domain_labels(key):
    domain_keys = jax.random.split(jax.random.fold_in(key, 5), N_DOM)

    def one_domain(domain_key):
        order = jax.random.permutation(domain_key, NODES_DEV).astype(jnp.int32)
        order = force_pair(order, 0, 0, True)
        order = force_pair(order, NODES_DEV - 1, 1, True)
        return order
    return jax.vmap(one_domain)(domain_keys)


def draw_connectivity(key, part):
    labels = domain_labels(key)
    table = jnp.asarray(natural_table())
    clipped = jnp.minimum(table, NODES_DEV - 1)

    def one_domain(label_row):
        return jnp.where(table < NODES_DEV, label_row[clipped], table)
    return jax.vmap(one_domain)(labels).reshape(CELLS, NODES_PER_CELL).astype(jnp.int32)


def draw_interface_nodes(key, part):
    labels = domain_labels(key)
    return labels[:, :IFACE].reshape(-1).astype(jnp.int32)


def level_of(stream_key, dims, shards, low, top_value):
    def one(position, shards_of):
        heights = jax.random.uniform(jax.random.fold_in(jax.random.fold_in(stream_key, 6), position), (shards_of,), jnp.float32, low / len(shards), top_value / len(shards))
        return jnp.repeat(jnp.exp(heights), dims[position] // shards_of).reshape((-1,) + (1,) * (len(dims) - position - 1))

    factor_of = one(*shards[0])
    for cut in shards[1:]:
        factor_of = factor_of * one(*cut)
    return factor_of


def bell_draw(stream_key, dims, deviation, reach, cuts=(), kind=jnp.bfloat16):
    result = jax.random.normal(stream_key, dims, jnp.float32) * deviation
    if len(cuts) > 0:
        result = level_of(stream_key, dims, cuts, -0.22, 0.18) * result
    return jnp.clip(result, min=-reach, max=reach).astype(kind)


def setup_inputs(seed: int = 0) -> dict:
    streams_of = jax.random.split(jax.random.key(seed), 8)
    return {
        "filter_input": bell_draw(streams_of[0], (NODES, STATES), 1.0, 6.0, ((0, 128), (1, 8))),
        "element_matrix": draw_element_matrix(jax.random.fold_in(streams_of[7], 71), 0),
        "cell_scale": jnp.clip(jnp.exp(math.log(2.0) - 1.3862944 * jax.random.uniform(streams_of[2], (CELLS,), jnp.float32) ** level_of(streams_of[2], (CELLS,), ((0, 128),), -0.2, 0.2)), 0.5, 2.0),
        "connectivity": draw_connectivity(jax.random.fold_in(streams_of[7], 71), 0),
        "interface_nodes": draw_interface_nodes(jax.random.fold_in(streams_of[7], 71), 0),
        "lumped_mass": jnp.clip(jnp.exp(math.log(2.0) - 1.3862944 * jax.random.uniform(streams_of[5], (NODES,), jnp.float32) ** level_of(streams_of[5], (NODES,), ((0, 128),), -0.2, 0.2)), 0.5, 2.0),
        "potential": jnp.clip(jax.random.uniform(streams_of[6], (NODES,), jnp.float32, -1.0, 1.0) * level_of(streams_of[6], (NODES,), ((0, 128),), -0.4, 0.0), -1.0, 1.0),
    }


filter_center = 5.0
filter_width = 6.0


def global_nodes(connectivity, interface_nodes):
    local = connectivity.reshape(N_DOM, CELLS_DEV * NODES_PER_CELL).astype(jnp.int32)
    shared = interface_nodes.reshape(N_DOM, IFACE).astype(jnp.int32)
    following = jnp.roll(shared, -1, axis=0)
    domains = jnp.arange(N_DOM, dtype=jnp.int32)[:, None]
    owned = domains * NODES_DEV + local
    offset = jnp.clip(local - NODES_DEV, 0, IFACE - 1).astype(jnp.int32)
    remote = ((domains + 1) % N_DOM) * NODES_DEV + jnp.take_along_axis(following, offset, axis=1)
    return jnp.where(local < NODES_DEV, owned, remote).astype(jnp.int32)


def apply_operator(values_in, element_matrix, cell_scale, node_index, lumped_mass, potential):
    kernel = element_matrix.astype(jnp.float32)
    scales = cell_scale.reshape(N_DOM, CELLS_DEV)

    def add_domain(summed, inputs):
        indices, weights = inputs
        gathered = values_in[indices].astype(jnp.float32).reshape(CELLS_DEV, NODES_PER_CELL, -1)
        products = jnp.einsum("ab,cbs->cas", kernel, gathered) * weights[:, None, None]
        summed = summed.at[indices].add(products.reshape(CELLS_DEV * NODES_PER_CELL, -1))
        return summed, None

    summed, unused = lax.scan(add_domain, jnp.zeros(values_in.shape, jnp.float32), (node_index, scales))
    return summed / lumped_mass[:, None] + potential[:, None] * values_in.astype(jnp.float32)


def reference(filter_input, element_matrix, cell_scale, connectivity, interface_nodes, lumped_mass, potential):
    node_index = global_nodes(connectivity, interface_nodes)
    blocks = filter_input.reshape(NODES, N_BAND, STATES_DEV).transpose(1, 0, 2)

    def filter_block(block):
        start_values = block.astype(jnp.float32)
        first_image = apply_operator(block, element_matrix, cell_scale, node_index, lumped_mass, potential)
        middle = ((first_image - filter_center * start_values) / filter_width).astype(jnp.bfloat16)
        second_image = apply_operator(middle, element_matrix, cell_scale, node_index, lumped_mass, potential)
        return (2.0 * (second_image - filter_center * middle.astype(jnp.float32)) / filter_width - start_values).astype(jnp.bfloat16)

    filtered_blocks = lax.map(filter_block, blocks)
    filtered = filtered_blocks.transpose(1, 0, 2).reshape(NODES, STATES)
    weighted = (filtered.astype(jnp.float32) * (lumped_mass / NODES)[:, None]).astype(jnp.bfloat16)
    intersection = jnp.dot(filtered.T, weighted, preferred_element_type=jnp.float32)
    return filtered, intersection
```

```python
import jax
import jax.numpy as jnp
from jax import lax
from jax.experimental import pallas as pl
from jax.experimental.pallas import tpu as pltpu
from jax.sharding import PartitionSpec as P

filter_center = 5.0
filter_width = 6.0

OWN = 1296
SHARED = 81
CELLS = 16
NPC = 125
STATES_DEV = 256
PAD = 128
OWN_PAD = 1408
INNER = 12
ENTRIES = CELLS * PAD
INNER_ENTRIES = INNER * PAD
OUTER_ENTRIES = ENTRIES - INNER_ENTRIES
IFACE_SLOT = 16
SLOTS = 24
BF = jnp.bfloat16
F32 = jnp.float32


def shifted(value, axis, steps):
    count = lax.axis_size(axis)
    pairs = [(source, (source + steps) % count) for source in range(count)]
    return lax.ppermute(value, axis, pairs)


def rows_match(column, width):
    lanes = lax.broadcasted_iota(jnp.int32, (column.shape[0], width), 1)
    return jnp.where(lanes == column, 1.0, 0.0).astype(BF)


def columns_match(row, start, height):
    places = lax.broadcasted_iota(jnp.int32, (height, row.shape[1]), 0)
    return jnp.where(places == row - start, 1.0, 0.0).astype(BF)


def dot(left, right):
    return jnp.dot(left, right, preferred_element_type=F32)


def two_parts(value):
    high = value.astype(BF)
    low = (value - high.astype(F32)).astype(BF)
    return high, low


def cell_products(gathered, element_ref, scale_ref, first_cell, out_ref, out_start):
    for pair in range(gathered.shape[0] // (2 * PAD)):
        block = gathered[pair * 2 * PAD : (pair + 1) * 2 * PAD]
        products = dot(element_ref[...], block)
        for half in range(2):
            scale = scale_ref[first_cell + 2 * pair + half]
            high, low = two_parts(products[half * PAD : (half + 1) * PAD] * scale)
            start = out_start + (2 * pair + half) * PAD
            out_ref[start : start + PAD, :STATES_DEV] = high
            out_ref[start : start + PAD, STATES_DEV:] = low


def inner_kernel(scale_ref, values_ref, index_t_ref, element_ref, terms_ref, outer_ref, padded, match):
    padded[:OWN, :] = values_ref[...]
    padded[OWN:, :] = jnp.zeros((OWN_PAD - OWN, STATES_DEV), BF)
    for group in range(4):
        for cell in range(4):
            number = group * 4 + cell
            match[cell * PAD : (cell + 1) * PAD, :] = rows_match(
                index_t_ref[:, number : number + 1], OWN_PAD
            )
        gathered = dot(match[...], padded[...]).astype(BF)
        if group < 3:
            cell_products(gathered, element_ref, scale_ref, group * 4, terms_ref, group * 4 * PAD)
        else:
            outer_ref[...] = gathered


def outer_kernel(
    scale_ref, outer_ref, remote_ref, index_ref, index_t_ref, element_ref, terms_ref, back_ref, held
):
    held[...] = jnp.zeros_like(held)
    held[:SHARED, :] = remote_ref[...]
    match = jnp.concatenate(
        [
            rows_match(index_t_ref[:, INNER + cell : INNER + cell + 1] - OWN, PAD)
            for cell in range(CELLS - INNER)
        ],
        axis=0,
    )
    gathered = (outer_ref[...].astype(F32) + dot(match, held[...])).astype(BF)
    cell_products(gathered, element_ref, scale_ref, INNER, terms_ref, 0)
    match = jnp.concatenate(
        [
            columns_match(index_ref[INNER + cell : INNER + cell + 1, :], OWN, PAD)
            for cell in range(CELLS - INNER)
        ],
        axis=1,
    )
    both = dot(match, terms_ref[...])
    back = (both[:, :STATES_DEV] + both[:, STATES_DEV:]).astype(BF)
    back_ref[...] = back[:SHARED, :]


def spread_kernel(inner_ref, outer_ref, index_ref, summed_ref, match):
    step = OWN // 3
    for tile in range(3):
        for cell in range(CELLS):
            match[:, cell * PAD : (cell + 1) * PAD] = columns_match(
                index_ref[cell : cell + 1, :], tile * step, step
            )
        both = dot(match[:, :INNER_ENTRIES], inner_ref[...]) + dot(
            match[:, INNER_ENTRIES:], outer_ref[...]
        )
        summed_ref[tile * step : (tile + 1) * step, :] = (
            both[:, :STATES_DEV] + both[:, STATES_DEV:]
        )


def with_returned(summed_ref, back_ref, index_ref, held):
    held[...] = jnp.zeros_like(held)
    held[:SHARED, :] = back_ref[...]
    match = columns_match(index_ref[IFACE_SLOT : IFACE_SLOT + 1, :], 0, OWN)
    return summed_ref[...] + dot(match, held[...])


def middle_kernel(
    summed_ref,
    back_ref,
    values_ref,
    mass_ref,
    potential_ref,
    index_ref,
    index_t_ref,
    middle_ref,
    shared_ref,
    held,
    padded,
):
    summed = with_returned(summed_ref, back_ref, index_ref, held)
    factor = 1.0 / (filter_width * mass_ref[...])
    own = (potential_ref[...] - filter_center) * (1.0 / filter_width)
    middle = (summed * factor + values_ref[...].astype(F32) * own).astype(BF)
    middle_ref[...] = middle
    padded[:OWN, :] = middle
    padded[OWN:, :] = jnp.zeros((OWN_PAD - OWN, STATES_DEV), BF)
    match = rows_match(index_t_ref[:, IFACE_SLOT : IFACE_SLOT + 1], OWN_PAD)
    shared_ref[...] = dot(match, padded[...]).astype(BF)[:SHARED, :]


def final_kernel(
    total_ref,
    summed_ref,
    back_ref,
    middle_ref,
    values_ref,
    mass_ref,
    potential_ref,
    index_ref,
    filtered_ref,
    weighted_ref,
    held,
):
    summed = with_returned(summed_ref, back_ref, index_ref, held)
    mass = mass_ref[...]
    factor = (2.0 / filter_width) / mass
    own = (potential_ref[...] - filter_center) * (2.0 / filter_width)
    filtered = (
        summed * factor + middle_ref[...].astype(F32) * own - values_ref[...].astype(F32)
    ).astype(BF)
    filtered_ref[...] = filtered
    weighted_ref[...] = (filtered.astype(F32) * (mass * total_ref[0])).astype(BF)


SCALARS = pl.BlockSpec(memory_space=pltpu.SMEM)
ARRAY = pl.BlockSpec(memory_space=pltpu.VMEM)
LIMIT = 40 * 1024 * 1024


def call(body, scalars, arrays, outs, scratch, flops, *args):
    return pl.pallas_call(
        body,
        out_shape=outs,
        in_specs=[SCALARS] * scalars + [ARRAY] * arrays,
        out_specs=[ARRAY] * len(outs),
        scratch_shapes=scratch,
        compiler_params=pltpu.CompilerParams(vmem_limit_bytes=LIMIT),
        cost_estimate=pl.CostEstimate(flops=flops, bytes_accessed=3_000_000, transcendentals=0),
    )(*args)


def shape(rows, columns, dtype):
    return jax.ShapeDtypeStruct((rows, columns), dtype)


def summed_terms(values, shared, scales, index, index_t, element):
    remote = shifted(shared, "dom", -1)
    inner, outer = call(
        inner_kernel,
        1,
        3,
        [shape(INNER_ENTRIES, 2 * STATES_DEV, BF), shape(OUTER_ENTRIES, STATES_DEV, BF)],
        [pltpu.VMEM((OWN_PAD, STATES_DEV), BF), pltpu.VMEM((4 * PAD, OWN_PAD), BF)],
        1_600_000_000,
        scales,
        values,
        index_t,
        element,
    )
    outer_terms, back = call(
        outer_kernel,
        1,
        5,
        [shape(OUTER_ENTRIES, 2 * STATES_DEV, BF), shape(SHARED, STATES_DEV, BF)],
        [pltpu.VMEM((PAD, STATES_DEV), BF)],
        200_000_000,
        scales,
        outer,
        remote,
        index,
        index_t,
        element,
    )
    returned = shifted(back, "dom", 1)
    (summed,) = call(
        spread_kernel,
        0,
        3,
        [shape(OWN, STATES_DEV, F32)],
        [pltpu.VMEM((OWN // 3, ENTRIES), BF)],
        2_700_000_000,
        inner,
        outer_terms,
        index,
    )
    return summed, returned


def filtered_states(
    filter_input, element_matrix, cell_scale, connectivity, interface_nodes, lumped_mass, potential
):
    shared = filter_input[interface_nodes]
    index = jnp.full((SLOTS, PAD), -1, jnp.int32)
    index = index.at[:CELLS, :NPC].set(connectivity)
    index = index.at[IFACE_SLOT, :SHARED].set(interface_nodes)
    index_t = index.T
    element = jnp.zeros((2 * PAD, 2 * PAD), BF)
    element = element.at[:NPC, :NPC].set(element_matrix)
    element = element.at[PAD : PAD + NPC, PAD : PAD + NPC].set(element_matrix)
    mass = lumped_mass[:, None]
    pot = potential[:, None]
    summed, returned = summed_terms(filter_input, shared, cell_scale, index, index_t, element)
    middle, shared = call(
        middle_kernel,
        0,
        7,
        [shape(OWN, STATES_DEV, BF), shape(SHARED, STATES_DEV, BF)],
        [pltpu.VMEM((PAD, STATES_DEV), BF), pltpu.VMEM((OWN_PAD, STATES_DEV), BF)],
        200_000_000,
        summed,
        returned,
        filter_input,
        mass,
        pot,
        index,
        index_t,
    )
    summed, returned = summed_terms(middle, shared, cell_scale, index, index_t, element)
    node_total = OWN * lax.axis_size("dom")
    total = jnp.full((1,), 1.0 / float(node_total), F32)
    return call(
        final_kernel,
        1,
        7,
        [shape(OWN, STATES_DEV, BF), shape(OWN, STATES_DEV, BF)],
        [pltpu.VMEM((PAD, STATES_DEV), BF)],
        200_000_000,
        total,
        summed,
        returned,
        middle,
        filter_input,
        mass,
        pot,
        index,
    )


def per_device(*args):
    filtered, weighted = filtered_states(*args)
    gathered = lax.all_gather(filtered, "band", axis=1, tiled=True)
    terms = lax.dot_general(
        gathered, weighted, (((0,), (0,)), ((), ())), preferred_element_type=jnp.float32
    ).astype(BF)
    domains = lax.axis_size("dom")
    pieces = lax.all_to_all(terms.reshape(domains, -1, terms.shape[1]), "dom", 0, 0)
    return filtered, jnp.sum(pieces.astype(F32), axis=0)


def solution(mesh):
    placed = (P("dom", "band"), P(), P("dom"), P("dom", None), P("dom"), P("dom"), P("dom"))
    return jax.shard_map(
        per_device,
        mesh=mesh,
        in_specs=placed,
        out_specs=(P("dom", "band"), P("dom", "band")),
        check_vma=False,
    )
```

```python
import jax
import jax.numpy as jnp
from jax import lax
from jax.experimental import pallas as pl
from jax.experimental.pallas import tpu as pltpu
from jax.sharding import PartitionSpec as P


filter_center = 5.0
filter_width = 6.0

OWN = 1296
SHARED = 81
CELLS = 16
NPC = 125
STATES_DEV = 256
PAD = 128
OWN_PAD = 1408
INNER = 12
ENTRIES = CELLS * PAD
INNER_ENTRIES = INNER * PAD
OUTER_ENTRIES = ENTRIES - INNER_ENTRIES
IFACE_SLOT = 16
SLOTS = 24
DOM = ("xh", "z", "y")
CHIPS = 4
BF = jnp.bfloat16
F32 = jnp.float32


def shifted(value, axis, steps):
    count = lax.axis_size(axis)
    pairs = [(source, (source + steps) % count) for source in range(count)]
    return lax.ppermute(value, axis, pairs)


def rows_match(column, width):
    lanes = lax.broadcasted_iota(jnp.int32, (column.shape[0], width), 1)
    return jnp.where(lanes == column, 1.0, 0.0).astype(BF)


def columns_match(row, start, height):
    places = lax.broadcasted_iota(jnp.int32, (height, row.shape[1]), 0)
    return jnp.where(places == row - start, 1.0, 0.0).astype(BF)


def dot(left, right):
    return jnp.dot(left, right, preferred_element_type=F32)


def two_parts(value):
    high = value.astype(BF)
    low = (value - high.astype(F32)).astype(BF)
    return high, low


def cell_products(gathered, element_ref, scale_ref, first_cell, out_ref, out_start):
    for pair in range(gathered.shape[0] // (2 * PAD)):
        block = gathered[pair * 2 * PAD : (pair + 1) * 2 * PAD]
        products = dot(element_ref[...], block)
        for half in range(2):
            scale = scale_ref[first_cell + 2 * pair + half]
            high, low = two_parts(products[half * PAD : (half + 1) * PAD] * scale)
            start = out_start + (2 * pair + half) * PAD
            out_ref[start : start + PAD, :STATES_DEV] = high
            out_ref[start : start + PAD, STATES_DEV:] = low


def pick_entries(scale_ref, values, index_t_ref, element_ref, terms_ref, outer_ref, match):
    for group in range(4):
        for cell in range(4):
            number = group * 4 + cell
            match[cell * PAD : (cell + 1) * PAD, :] = rows_match(
                index_t_ref[:, number : number + 1], OWN_PAD
            )
        gathered = dot(match[...], values[...]).astype(BF)
        if group < 3:
            cell_products(gathered, element_ref, scale_ref, group * 4, terms_ref, group * 4 * PAD)
        else:
            outer_ref[...] = gathered


def pad_values(padded, values):
    padded[:OWN, :] = values
    padded[OWN:, :] = jnp.zeros((OWN_PAD - OWN, STATES_DEV), BF)


def first_kernel(
    scale_ref,
    values_ref,
    cells_ref,
    nodes_ref,
    matrix_ref,
    terms_ref,
    outer_ref,
    shared_ref,
    index_ref,
    index_t_ref,
    element_ref,
    padded,
    match,
    table,
):
    table[...] = jnp.full((PAD, PAD), -1, jnp.int32)
    table[:CELLS, :NPC] = cells_ref[...]
    table[IFACE_SLOT : IFACE_SLOT + 1, :SHARED] = nodes_ref[...]
    index_ref[...] = table[:SLOTS, :]
    index_t_ref[...] = jnp.transpose(table[...])
    element_ref[...] = jnp.zeros_like(element_ref)
    element_ref[:NPC, :NPC] = matrix_ref[...]
    element_ref[PAD : PAD + NPC, PAD : PAD + NPC] = matrix_ref[...]
    pad_values(padded, values_ref[...])
    chosen = rows_match(index_t_ref[:, IFACE_SLOT : IFACE_SLOT + 1], OWN_PAD)
    shared_ref[...] = dot(chosen, padded[...]).astype(BF)[:SHARED, :]
    pick_entries(scale_ref, padded, index_t_ref, element_ref, terms_ref, outer_ref, match)


def inner_kernel(scale_ref, values_ref, index_t_ref, element_ref, terms_ref, outer_ref, padded, match):
    pad_values(padded, values_ref[...])
    pick_entries(scale_ref, padded, index_t_ref, element_ref, terms_ref, outer_ref, match)


def outer_kernel(
    scale_ref, outer_ref, remote_ref, index_ref, index_t_ref, element_ref, terms_ref, back_ref, held
):
    held[...] = jnp.zeros_like(held)
    held[:SHARED, :] = remote_ref[...]
    match = jnp.concatenate(
        [
            rows_match(index_t_ref[:, INNER + cell : INNER + cell + 1] - OWN, PAD)
            for cell in range(CELLS - INNER)
        ],
        axis=0,
    )
    gathered = (outer_ref[...].astype(F32) + dot(match, held[...])).astype(BF)
    cell_products(gathered, element_ref, scale_ref, INNER, terms_ref, 0)
    match = jnp.concatenate(
        [
            columns_match(index_ref[INNER + cell : INNER + cell + 1, :], OWN, PAD)
            for cell in range(CELLS - INNER)
        ],
        axis=1,
    )
    both = dot(match, terms_ref[...])
    back = (both[:, :STATES_DEV] + both[:, STATES_DEV:]).astype(BF)
    back_ref[...] = back[:SHARED, :]


def spread_kernel(inner_ref, outer_ref, index_ref, summed_ref, match):
    step = OWN // 3
    for tile in range(3):
        for cell in range(CELLS):
            match[:, cell * PAD : (cell + 1) * PAD] = columns_match(
                index_ref[cell : cell + 1, :], tile * step, step
            )
        both = dot(match[:, :INNER_ENTRIES], inner_ref[...]) + dot(
            match[:, INNER_ENTRIES:], outer_ref[...]
        )
        summed_ref[tile * step : (tile + 1) * step, :] = (
            both[:, :STATES_DEV] + both[:, STATES_DEV:]
        )


def with_returned(summed_ref, back_ref, index_ref, held):
    held[...] = jnp.zeros_like(held)
    held[:SHARED, :] = back_ref[...]
    match = columns_match(index_ref[IFACE_SLOT : IFACE_SLOT + 1, :], 0, OWN)
    return summed_ref[...] + dot(match, held[...])


def middle_kernel(
    summed_ref,
    back_ref,
    values_ref,
    mass_ref,
    potential_ref,
    index_ref,
    index_t_ref,
    middle_ref,
    shared_ref,
    held,
    padded,
):
    summed = with_returned(summed_ref, back_ref, index_ref, held)
    factor = 1.0 / (filter_width * mass_ref[...])
    own = (potential_ref[...] - filter_center) * (1.0 / filter_width)
    middle = (summed * factor + values_ref[...].astype(F32) * own).astype(BF)
    middle_ref[...] = middle
    pad_values(padded, middle)
    match = rows_match(index_t_ref[:, IFACE_SLOT : IFACE_SLOT + 1], OWN_PAD)
    shared_ref[...] = dot(match, padded[...]).astype(BF)[:SHARED, :]


def final_kernel(
    total_ref,
    summed_ref,
    back_ref,
    middle_ref,
    values_ref,
    mass_ref,
    potential_ref,
    index_ref,
    filtered_ref,
    weighted_ref,
    held,
):
    summed = with_returned(summed_ref, back_ref, index_ref, held)
    mass = mass_ref[...]
    factor = (2.0 / filter_width) / mass
    own = (potential_ref[...] - filter_center) * (2.0 / filter_width)
    filtered = (
        summed * factor + middle_ref[...].astype(F32) * own - values_ref[...].astype(F32)
    ).astype(BF)
    filtered_ref[...] = filtered
    weighted_ref[...] = (filtered.astype(F32) * (mass * total_ref[0])).astype(BF)


SCALARS = pl.BlockSpec(memory_space=pltpu.SMEM)
ARRAY = pl.BlockSpec(memory_space=pltpu.VMEM)
LIMIT = 40 * 1024 * 1024


def call(body, scalars, arrays, outs, scratch, flops, *args):
    return pl.pallas_call(
        body,
        out_shape=outs,
        in_specs=[SCALARS] * scalars + [ARRAY] * arrays,
        out_specs=[ARRAY] * len(outs),
        scratch_shapes=scratch,
        compiler_params=pltpu.CompilerParams(vmem_limit_bytes=LIMIT),
        cost_estimate=pl.CostEstimate(flops=flops, bytes_accessed=3_000_000, transcendentals=0),
    )(*args)


def shape(rows, columns, dtype):
    return jax.ShapeDtypeStruct((rows, columns), dtype)


INNER_OUTS = [shape(INNER_ENTRIES, 2 * STATES_DEV, BF), shape(OUTER_ENTRIES, STATES_DEV, BF)]
INNER_SCRATCH = [pltpu.VMEM((OWN_PAD, STATES_DEV), BF), pltpu.VMEM((4 * PAD, OWN_PAD), BF)]


def summed_terms(inner, outer, remote, scales, index, index_t, element):
    outer_terms, back = call(
        outer_kernel,
        1,
        5,
        [shape(OUTER_ENTRIES, 2 * STATES_DEV, BF), shape(SHARED, STATES_DEV, BF)],
        [pltpu.VMEM((PAD, STATES_DEV), BF)],
        200_000_000,
        scales,
        outer,
        remote,
        index,
        index_t,
        element,
    )
    returned = shifted(back, DOM, 1)
    (summed,) = call(
        spread_kernel,
        0,
        3,
        [shape(OWN, STATES_DEV, F32)],
        [pltpu.VMEM((OWN // 3, ENTRIES), BF)],
        2_700_000_000,
        inner,
        outer_terms,
        index,
    )
    return summed, returned


def filtered_states(
    filter_input, element_matrix, cell_scale, connectivity, interface_nodes, lumped_mass, potential
):
    inner, outer, shared, index, index_t, element = call(
        first_kernel,
        1,
        4,
        INNER_OUTS
        + [
            shape(SHARED, STATES_DEV, BF),
            shape(SLOTS, PAD, jnp.int32),
            shape(PAD, PAD, jnp.int32),
            shape(2 * PAD, 2 * PAD, BF),
        ],
        INNER_SCRATCH + [pltpu.VMEM((PAD, PAD), jnp.int32)],
        1_800_000_000,
        cell_scale,
        filter_input,
        connectivity,
        interface_nodes[None, :],
        element_matrix,
    )
    mass = lumped_mass[:, None]
    pot = potential[:, None]
    remote = shifted(shared, DOM, -1)
    summed, returned = summed_terms(inner, outer, remote, cell_scale, index, index_t, element)
    middle, shared = call(
        middle_kernel,
        0,
        7,
        [shape(OWN, STATES_DEV, BF), shape(SHARED, STATES_DEV, BF)],
        [pltpu.VMEM((PAD, STATES_DEV), BF), pltpu.VMEM((OWN_PAD, STATES_DEV), BF)],
        200_000_000,
        summed,
        returned,
        filter_input,
        mass,
        pot,
        index,
        index_t,
    )
    remote = shifted(shared, DOM, -1)
    inner, outer = call(
        inner_kernel,
        1,
        3,
        INNER_OUTS,
        INNER_SCRATCH,
        1_600_000_000,
        cell_scale,
        middle,
        index_t,
        element,
    )
    summed, returned = summed_terms(inner, outer, remote, cell_scale, index, index_t, element)
    node_total = OWN * lax.axis_size(DOM)
    total = jnp.full((1,), 1.0 / float(node_total), F32)
    return call(
        final_kernel,
        1,
        7,
        [shape(OWN, STATES_DEV, BF), shape(OWN, STATES_DEV, BF)],
        [pltpu.VMEM((PAD, STATES_DEV), BF)],
        200_000_000,
        total,
        summed,
        returned,
        middle,
        filter_input,
        mass,
        pot,
        index,
    )


HELD = ((0, 1, 2, 3), (1, 2, 0, 3), (2, 1, 3, 0), (3, 2, 1, 0))


def moved(value, axis, pairs):
    return lax.ppermute(value, axis, pairs)


def collect_kernel(place_ref, first_ref, second_ref, out_ref):
    for number in range(8):
        ref = first_ref if number < 4 else second_ref
        terms = ref[:, number % 4].astype(F32)
        out_ref[place_ref[number]] = jnp.sum(terms, axis=0).astype(BF)


def block_terms(block, weights):
    terms = lax.dot_general(
        block, weights, (((0,), (0,)), ((), ())), preferred_element_type=jnp.float32
    ).astype(BF)
    return terms[:, :STATES_DEV], terms[:, STATES_DEV:]


def by_line(pieces):
    lines = lax.axis_size("y")
    height = STATES_DEV * lax.axis_size("xl") * lax.axis_size("c") // lax.axis_size(DOM)
    rows = [p.reshape(-1, lines, height, STATES_DEV) for p in pieces]
    rows = jnp.concatenate(rows, axis=0)
    rows = rows.reshape(len(pieces), -1, lines, height, STATES_DEV)
    return rows.transpose(2, 0, 1, 3, 4)


def over_y(sent):
    return lax.all_to_all(sent, "y", 0, 0)


def after(value, earlier):
    return lax.optimization_barrier((value, earlier))[0]


def intersection_tile(filtered, weighted):
    chip = lax.axis_index("xl")
    core = lax.axis_index("c")
    swap = [(0, 1), (1, 0)]
    right_1 = moved(filtered, "xl", [(0, 1), (1, 2), (2, 3)])
    left_1 = moved(filtered, "xl", [(1, 0), (2, 1), (3, 2)])
    weights = jnp.concatenate([weighted, moved(weighted, "c", swap)], axis=1)
    mine_0, theirs_0 = block_terms(filtered, weights)
    right_2 = moved(right_1, "xl", [(1, 2), (2, 3)])
    left_2 = moved(left_1, "xl", [(1, 0), (2, 1)])
    mine_1, theirs_1 = block_terms(jnp.where(chip < 2, left_1, right_1), weights)
    swapped = moved(jnp.concatenate([theirs_0, theirs_1], axis=0), "c", swap)
    sent = by_line([mine_0, swapped[:STATES_DEV], mine_1, swapped[STATES_DEV:]])
    first = over_y(sent)
    passed = jnp.where(chip == 1, left_2, right_2)
    relayed = moved(passed, "xl", [(1, 0), (2, 3)])
    slot_2 = jnp.where(
        chip == 0, left_2, jnp.where(chip == 1, right_1, jnp.where(chip == 2, left_1, right_2))
    )
    mine_2, theirs_2 = block_terms(after(slot_2, sent), weights)
    swapped_2 = moved(theirs_2, "c", swap)
    slot_3 = jnp.where((chip == 1) | (chip == 2), passed, relayed)
    mine_3, theirs_3 = block_terms(after(slot_3, sent), weights)
    swapped_3 = moved(theirs_3, "c", swap)
    second = over_y(by_line([mine_2, swapped_2, mine_3, swapped_3]))
    blocks = jnp.asarray(HELD, jnp.int32)[chip]
    place = jnp.stack([2 * blocks + core, 2 * blocks + 1 - core], axis=1).reshape(-1)
    kept = pl.pallas_call(
        collect_kernel,
        out_shape=jax.ShapeDtypeStruct((8,) + first.shape[2:], BF),
        in_specs=[SCALARS, ARRAY, ARRAY],
        out_specs=ARRAY,
        compiler_params=pltpu.CompilerParams(vmem_limit_bytes=LIMIT),
    )(place.astype(jnp.int32), first, second)
    planes = lax.axis_size(("xh", "z"))
    pieces = lax.all_to_all(kept.reshape(planes, -1, STATES_DEV), ("xh", "z"), 0, 0)
    return jnp.sum(pieces.astype(F32), axis=0)


def per_device(*args):
    filtered, weighted = filtered_states(*args)
    tile = intersection_tile(filtered, weighted)
    return filtered, tile


def solution(mesh):
    fine = jax.sharding.Mesh(
        mesh.devices.reshape(2, 8, 8, CHIPS, 2), ("xh", "z", "y", "xl", "c")
    )
    band = ("xl", "c")
    placed = (P(DOM, band), P(), P(DOM), P(DOM, None), P(DOM), P(DOM), P(DOM))
    return jax.shard_map(
        per_device,
        mesh=fine,
        in_specs=placed,
        out_specs=(P(DOM, band), P(DOM, band)),
        check_vma=False,
    )
```

```python
import jax
import jax.numpy as jnp
from jax import lax
from jax.experimental import pallas as pl
from jax.experimental.pallas import tpu as pltpu
from jax.sharding import PartitionSpec as P


filter_center = 5.0
filter_width = 6.0

OWN = 1296
SHARED = 81
CELLS = 16
NPC = 125
STATES_DEV = 256
PAD = 128
OWN_PAD = 1408
INNER = 12
ENTRIES = CELLS * PAD
INNER_ENTRIES = INNER * PAD
OUTER_ENTRIES = ENTRIES - INNER_ENTRIES
IFACE_SLOT = 16
SLOTS = 24
DOM = ("xh", "z", "y")
CHIPS = 4
BF = jnp.bfloat16
F32 = jnp.float32


def shifted(value, axis, steps):
    count = lax.axis_size(axis)
    pairs = [(source, (source + steps) % count) for source in range(count)]
    return lax.ppermute(value, axis, pairs)


def rows_match(column, width):
    lanes = lax.broadcasted_iota(jnp.int32, (column.shape[0], width), 1)
    return jnp.where(lanes == column, 1.0, 0.0).astype(BF)


def columns_match(row, start, height):
    places = lax.broadcasted_iota(jnp.int32, (height, row.shape[1]), 0)
    return jnp.where(places == row - start, 1.0, 0.0).astype(BF)


def dot(left, right):
    return jnp.dot(left, right, preferred_element_type=F32)


def two_parts(value):
    high = value.astype(BF)
    low = (value - high.astype(F32)).astype(BF)
    return high, low


def cell_products(gathered, element_ref, scale_ref, first_cell, out_ref, out_start):
    for pair in range(gathered.shape[0] // (2 * PAD)):
        block = gathered[pair * 2 * PAD : (pair + 1) * 2 * PAD]
        products = dot(element_ref[...], block)
        for half in range(2):
            scale = scale_ref[first_cell + 2 * pair + half]
            high, low = two_parts(products[half * PAD : (half + 1) * PAD] * scale)
            start = out_start + (2 * pair + half) * PAD
            out_ref[start : start + PAD, :STATES_DEV] = high
            out_ref[start : start + PAD, STATES_DEV:] = low


def pick_entries(scale_ref, values, index_t_ref, element_ref, terms_ref, outer_ref, match):
    for group in range(4):
        for cell in range(4):
            number = group * 4 + cell
            match[cell * PAD : (cell + 1) * PAD, :] = rows_match(
                index_t_ref[:, number : number + 1], OWN_PAD
            )
        gathered = dot(match[...], values[...]).astype(BF)
        if group < 3:
            cell_products(gathered, element_ref, scale_ref, group * 4, terms_ref, group * 4 * PAD)
        else:
            outer_ref[...] = gathered


def pad_values(padded, values):
    padded[:OWN, :] = values
    padded[OWN:, :] = jnp.zeros((OWN_PAD - OWN, STATES_DEV), BF)


def first_kernel(
    scale_ref,
    values_ref,
    cells_ref,
    nodes_ref,
    matrix_ref,
    terms_ref,
    outer_ref,
    shared_ref,
    index_ref,
    index_t_ref,
    element_ref,
    padded,
    match,
    table,
):
    table[...] = jnp.full((PAD, PAD), -1, jnp.int32)
    table[:CELLS, :NPC] = cells_ref[...]
    table[IFACE_SLOT : IFACE_SLOT + 1, :SHARED] = nodes_ref[...]
    index_ref[...] = table[:SLOTS, :]
    index_t_ref[...] = jnp.transpose(table[...])
    element_ref[...] = jnp.zeros_like(element_ref)
    element_ref[:NPC, :NPC] = matrix_ref[...]
    element_ref[PAD : PAD + NPC, PAD : PAD + NPC] = matrix_ref[...]
    pad_values(padded, values_ref[...])
    chosen = rows_match(index_t_ref[:, IFACE_SLOT : IFACE_SLOT + 1], OWN_PAD)
    shared_ref[...] = dot(chosen, padded[...]).astype(BF)[:SHARED, :]
    pick_entries(scale_ref, padded, index_t_ref, element_ref, terms_ref, outer_ref, match)


def inner_kernel(scale_ref, values_ref, index_t_ref, element_ref, terms_ref, outer_ref, padded, match):
    pad_values(padded, values_ref[...])
    pick_entries(scale_ref, padded, index_t_ref, element_ref, terms_ref, outer_ref, match)


def outer_kernel(
    scale_ref, outer_ref, remote_ref, index_ref, index_t_ref, element_ref, terms_ref, back_ref, held
):
    held[...] = jnp.zeros_like(held)
    held[:SHARED, :] = remote_ref[...]
    match = jnp.concatenate(
        [
            rows_match(index_t_ref[:, INNER + cell : INNER + cell + 1] - OWN, PAD)
            for cell in range(CELLS - INNER)
        ],
        axis=0,
    )
    gathered = (outer_ref[...].astype(F32) + dot(match, held[...])).astype(BF)
    cell_products(gathered, element_ref, scale_ref, INNER, terms_ref, 0)
    match = jnp.concatenate(
        [
            columns_match(index_ref[INNER + cell : INNER + cell + 1, :], OWN, PAD)
            for cell in range(CELLS - INNER)
        ],
        axis=1,
    )
    both = dot(match, terms_ref[...])
    back = (both[:, :STATES_DEV] + both[:, STATES_DEV:]).astype(BF)
    back_ref[...] = back[:SHARED, :]


def spread_kernel(inner_ref, outer_ref, index_ref, summed_ref, match):
    step = OWN // 3
    for tile in range(3):
        for cell in range(CELLS):
            match[:, cell * PAD : (cell + 1) * PAD] = columns_match(
                index_ref[cell : cell + 1, :], tile * step, step
            )
        both = dot(match[:, :INNER_ENTRIES], inner_ref[...]) + dot(
            match[:, INNER_ENTRIES:], outer_ref[...]
        )
        summed_ref[tile * step : (tile + 1) * step, :] = (
            both[:, :STATES_DEV] + both[:, STATES_DEV:]
        )


def with_returned(summed_ref, back_ref, index_ref, held):
    held[...] = jnp.zeros_like(held)
    held[:SHARED, :] = back_ref[...]
    match = columns_match(index_ref[IFACE_SLOT : IFACE_SLOT + 1, :], 0, OWN)
    return summed_ref[...] + dot(match, held[...])


def middle_kernel(
    summed_ref,
    back_ref,
    values_ref,
    mass_ref,
    potential_ref,
    index_ref,
    index_t_ref,
    middle_ref,
    shared_ref,
    held,
    padded,
):
    summed = with_returned(summed_ref, back_ref, index_ref, held)
    factor = 1.0 / (filter_width * mass_ref[...])
    own = (potential_ref[...] - filter_center) * (1.0 / filter_width)
    middle = (summed * factor + values_ref[...].astype(F32) * own).astype(BF)
    middle_ref[...] = middle
    pad_values(padded, middle)
    match = rows_match(index_t_ref[:, IFACE_SLOT : IFACE_SLOT + 1], OWN_PAD)
    shared_ref[...] = dot(match, padded[...]).astype(BF)[:SHARED, :]


def final_kernel(
    total_ref,
    summed_ref,
    back_ref,
    middle_ref,
    values_ref,
    mass_ref,
    potential_ref,
    index_ref,
    filtered_ref,
    weighted_ref,
    held,
):
    summed = with_returned(summed_ref, back_ref, index_ref, held)
    mass = mass_ref[...]
    factor = (2.0 / filter_width) / mass
    own = (potential_ref[...] - filter_center) * (2.0 / filter_width)
    filtered = (
        summed * factor + middle_ref[...].astype(F32) * own - values_ref[...].astype(F32)
    ).astype(BF)
    filtered_ref[...] = filtered
    weighted_ref[...] = (filtered.astype(F32) * (mass * total_ref[0])).astype(BF)


SCALARS = pl.BlockSpec(memory_space=pltpu.SMEM)
ARRAY = pl.BlockSpec(memory_space=pltpu.VMEM)
LIMIT = 40 * 1024 * 1024


def call(body, scalars, arrays, outs, scratch, flops, *args):
    return pl.pallas_call(
        body,
        out_shape=outs,
        in_specs=[SCALARS] * scalars + [ARRAY] * arrays,
        out_specs=[ARRAY] * len(outs),
        scratch_shapes=scratch,
        compiler_params=pltpu.CompilerParams(vmem_limit_bytes=LIMIT),
        cost_estimate=pl.CostEstimate(flops=flops, bytes_accessed=3_000_000, transcendentals=0),
    )(*args)


def shape(rows, columns, dtype):
    return jax.ShapeDtypeStruct((rows, columns), dtype)


INNER_OUTS = [shape(INNER_ENTRIES, 2 * STATES_DEV, BF), shape(OUTER_ENTRIES, STATES_DEV, BF)]
INNER_SCRATCH = [pltpu.VMEM((OWN_PAD, STATES_DEV), BF), pltpu.VMEM((4 * PAD, OWN_PAD), BF)]


def summed_terms(inner, outer, remote, scales, index, index_t, element):
    outer_terms, back = call(
        outer_kernel,
        1,
        5,
        [shape(OUTER_ENTRIES, 2 * STATES_DEV, BF), shape(SHARED, STATES_DEV, BF)],
        [pltpu.VMEM((PAD, STATES_DEV), BF)],
        200_000_000,
        scales,
        outer,
        remote,
        index,
        index_t,
        element,
    )
    returned = shifted(back, DOM, 1)
    (summed,) = call(
        spread_kernel,
        0,
        3,
        [shape(OWN, STATES_DEV, F32)],
        [pltpu.VMEM((OWN // 3, ENTRIES), BF)],
        2_700_000_000,
        inner,
        outer_terms,
        index,
    )
    return summed, returned


def filtered_states(
    filter_input, element_matrix, cell_scale, connectivity, interface_nodes, lumped_mass, potential
):
    inner, outer, shared, index, index_t, element = call(
        first_kernel,
        1,
        4,
        INNER_OUTS
        + [
            shape(SHARED, STATES_DEV, BF),
            shape(SLOTS, PAD, jnp.int32),
            shape(PAD, PAD, jnp.int32),
            shape(2 * PAD, 2 * PAD, BF),
        ],
        INNER_SCRATCH + [pltpu.VMEM((PAD, PAD), jnp.int32)],
        1_800_000_000,
        cell_scale,
        filter_input,
        connectivity,
        interface_nodes[None, :],
        element_matrix,
    )
    mass = lumped_mass[:, None]
    pot = potential[:, None]
    remote = shifted(shared, DOM, -1)
    summed, returned = summed_terms(inner, outer, remote, cell_scale, index, index_t, element)
    middle, shared = call(
        middle_kernel,
        0,
        7,
        [shape(OWN, STATES_DEV, BF), shape(SHARED, STATES_DEV, BF)],
        [pltpu.VMEM((PAD, STATES_DEV), BF), pltpu.VMEM((OWN_PAD, STATES_DEV), BF)],
        200_000_000,
        summed,
        returned,
        filter_input,
        mass,
        pot,
        index,
        index_t,
    )
    remote = shifted(shared, DOM, -1)
    inner, outer = call(
        inner_kernel,
        1,
        3,
        INNER_OUTS,
        INNER_SCRATCH,
        1_600_000_000,
        cell_scale,
        middle,
        index_t,
        element,
    )
    summed, returned = summed_terms(inner, outer, remote, cell_scale, index, index_t, element)
    node_total = OWN * lax.axis_size(DOM)
    total = jnp.full((1,), 1.0 / float(node_total), F32)
    return call(
        final_kernel,
        1,
        7,
        [shape(OWN, STATES_DEV, BF), shape(OWN, STATES_DEV, BF)],
        [pltpu.VMEM((PAD, STATES_DEV), BF)],
        200_000_000,
        total,
        summed,
        returned,
        middle,
        filter_input,
        mass,
        pot,
        index,
    )


HELD = ((0, 1, 2, 3), (1, 2, 0, 3), (2, 1, 3, 0), (3, 2, 1, 0))


def moved(value, axis, pairs):
    return lax.ppermute(value, axis, pairs)


def collect_kernel(place_ref, first_ref, second_ref, third_ref, out_ref):
    pieces = [(first_ref, piece) for piece in range(4)]
    pieces += [(second_ref, piece) for piece in range(2)]
    pieces += [(third_ref, piece) for piece in range(2)]
    for number, (ref, piece) in enumerate(pieces):
        terms = ref[:, piece].astype(F32)
        out_ref[place_ref[number]] = jnp.sum(terms, axis=0).astype(BF)


def block_terms(block, weights):
    terms = lax.dot_general(
        block, weights, (((0,), (0,)), ((), ())), preferred_element_type=jnp.float32
    ).astype(BF)
    return terms[:, :STATES_DEV], terms[:, STATES_DEV:]


def by_line(pieces):
    lines = lax.axis_size("y")
    height = STATES_DEV * lax.axis_size("xl") * lax.axis_size("c") // lax.axis_size(DOM)
    rows = [p.reshape(-1, lines, height, STATES_DEV) for p in pieces]
    rows = jnp.concatenate(rows, axis=0)
    rows = rows.reshape(len(pieces), -1, lines, height, STATES_DEV)
    return rows.transpose(2, 0, 1, 3, 4)


def over_y(sent):
    return lax.all_to_all(sent, "y", 0, 0)


def after(value, earlier):
    return lax.optimization_barrier((value, earlier))[0]


def intersection_tile(filtered, weighted):
    chip = lax.axis_index("xl")
    core = lax.axis_index("c")
    swap = [(0, 1), (1, 0)]
    right_1 = moved(filtered, "xl", [(0, 1), (1, 2), (2, 3)])
    left_1 = moved(filtered, "xl", [(1, 0), (2, 1), (3, 2)])
    other = moved(weighted, "c", swap)
    weights = jnp.concatenate([weighted, other], axis=1)
    mine_0, theirs_0 = block_terms(filtered, weights)
    right_2 = moved(right_1, "xl", [(1, 2), (2, 3)])
    left_2 = moved(left_1, "xl", [(1, 0), (2, 1)])
    mine_1, theirs_1 = block_terms(jnp.where(chip < 2, left_1, right_1), weights)
    swapped = moved(jnp.concatenate([theirs_0, theirs_1], axis=0), "c", swap)
    sent = by_line([mine_0, swapped[:STATES_DEV], mine_1, swapped[STATES_DEV:]])
    first = over_y(sent)
    passed = jnp.where(chip == 1, left_2, right_2)
    relayed = moved(passed, "xl", [(1, 0), (2, 3)])
    left_2, right_2, passed = lax.optimization_barrier((left_2, right_2, passed))
    slot_2 = jnp.where(
        chip == 0, left_2, jnp.where(chip == 1, right_1, jnp.where(chip == 2, left_1, right_2))
    )
    mine_2, theirs_2 = block_terms(after(slot_2, sent), weights)
    swapped = moved(theirs_2, "c", swap)
    sent = by_line([mine_2, swapped])
    second = over_y(sent)
    slot_3 = jnp.where((chip == 1) | (chip == 2), passed, relayed)
    mine_3, theirs_3 = block_terms(after(slot_3, sent), weights)
    swapped = moved(theirs_3, "c", swap)
    third = over_y(by_line([mine_3, swapped]))
    blocks = jnp.asarray(HELD, jnp.int32)[chip]
    place = jnp.stack([2 * blocks + core, 2 * blocks + 1 - core], axis=1).reshape(-1)
    kept = pl.pallas_call(
        collect_kernel,
        out_shape=jax.ShapeDtypeStruct((8,) + first.shape[2:], BF),
        in_specs=[SCALARS, ARRAY, ARRAY, ARRAY],
        out_specs=ARRAY,
        compiler_params=pltpu.CompilerParams(vmem_limit_bytes=LIMIT),
    )(place.astype(jnp.int32), first, second, third)
    planes = lax.axis_size(("xh", "z"))
    pieces = lax.all_to_all(kept.reshape(planes, -1, STATES_DEV), ("xh", "z"), 0, 0)
    return jnp.sum(pieces.astype(F32), axis=0)


def per_device(*args):
    filtered, weighted = filtered_states(*args)
    tile = intersection_tile(filtered, weighted)
    return filtered, tile


def solution(mesh):
    fine = jax.sharding.Mesh(
        mesh.devices.reshape(2, 8, 8, CHIPS, 2), ("xh", "z", "y", "xl", "c")
    )
    band = ("xl", "c")
    placed = (P(DOM, band), P(), P(DOM), P(DOM, None), P(DOM), P(DOM), P(DOM))
    return jax.shard_map(
        per_device,
        mesh=fine,
        in_specs=placed,
        out_specs=(P(DOM, band), P(DOM, band)),
        check_vma=False,
    )
```
